32 devices in a mesh: layer: 4 (over z), tile: 8 (over y, x, core).
Axes of the slice: x: 2, y: 2, z: 4, core: 2. Of those that a mesh axis runs over, the one named last changes fastest.
Arguments:
- leaf_rhs: float32 [4, 32, 128, 256], P('layer', 'tile'), may hold values from -6 to 6
- leaf_inv: float32 [4, 32, 128, 128], P('layer', 'tile'), as said below
- par_rhs: float32 [4, 16, 128, 256], P('layer', 'tile'), may hold values from -6 to 6
- par_inv: float32 [4, 16, 128, 128], P('layer', 'tile'), as said below
- top_rhs: float32 [16, 128, 256], P('tile', None, 'layer'), may hold values from -6 to 6
- top_inv: float32 [16, 128, 128], P('tile'), as said below
- leaf_tiles: float32 [4, 1280, 128, 128], P('layer', 'tile'), may hold values from -0.125 to 0.125
- leaf_cols: int32 [4, 1280], P('layer', 'tile'), may hold values from 0 to 3
- leaf_rows: int32 [4, 1280], P('layer', 'tile'), may hold values from 0 to 31, as said below
- leaf_count: int32 [4, 8], P('layer', 'tile'), may hold values from 1 to 160, as said below
- par_tiles: float32 [4, 640, 128, 128], P('layer', 'tile'), may hold values from -0.125 to 0.125
- par_cols: int32 [4, 640], P('layer', 'tile'), may hold values from 0 to 1
- par_rows: int32 [4, 640], P('layer', 'tile'), may hold values from 0 to 15
- par_count: int32 [4, 8], P('layer', 'tile'), may hold values from 1 to 80, as said below
Outputs:
- parent_solution: float32 [4, 16, 128, 256], P('layer', 'tile')
- top_solution: float32 [16, 128, 256], P('tile', None, 'layer')
The draws below stay inside these ranges and needn't reach their ends.
Inputs may be any that keep to these rules, and one draw needn't show every extreme that they name: `leaf_inv`: lower triangular, diagonal entries of magnitude 0.5 to 2. `par_inv`: lower triangular, diagonal entries of magnitude 0.5 to 2. `top_inv`: lower triangular, diagonal entries of magnitude 0.5 to 2. `leaf_rows`: the elimination subtree of a lower-level supernode of owner o lies in o's group of owners: owners o and q share a group when o // 2 % (1) equals q // 2 % 1; a tile below 16 names an upper-level supernode held by an owner of the same group, and the top-level supernodes are ancestors of every subtree. `leaf_count`: some owner of every layer has a full list. `par_count`: some owner of every layer has a full list.
All inputs are finite; a program needn't handle non-finite values.
Results may differ from the reference program's by a relative error of at most 0.0003.
Values sent between devices are 32-bit elements; how exact they have to be, the bound alone decides.
No kernel may reach another device: no remote copies, remote signals or barrier semaphores. Data moves between devices by JAX's collectives and lax.ppermute only.
A program may use at most 128 MiB of HBM per device.

```python
import jax
import jax.numpy as jnp
from jax import lax

BS = 128
NRHS = 256
LEAF_DEV = 4
PAR_DEV = 2
LT_DEV = 160
PT_DEV = 80
LAYERS = 4
OWNERS = 8
LEAVES = 32
PARENTS = 16
TOP = 16
LT_ALL = 1280
PT_ALL = 640


def lower_blocks(key, number):
    first, second, third = jax.random.split(key, 3)
    diagonal = jax.random.uniform(first, (number, BS), jnp.float32, 0.5, 2.0)
    spread = 0.6
    lower = jax.random.normal(second, (number, BS, BS), jnp.float32) * (spread / BS ** 0.5)
    lower = jnp.tril(lower, -1)
    sign = jnp.where(jax.random.bernoulli(third, 0.5, (number, BS)), 1.0, -1.0)
    eye = jnp.eye(BS, dtype=jnp.float32)
    return lower + eye[None] * (diagonal * sign)[:, :, None]


def list_counts(key, most):
    first, second = jax.random.split(key)
    shifts = jax.random.randint(first, (LAYERS, OWNERS), 0, 4)
    counts = jnp.maximum(jnp.right_shift(jnp.full((LAYERS, OWNERS), most, jnp.int32), shifts), 1)
    full_owner = jax.random.randint(second, (LAYERS, 1), 0, OWNERS)
    owner_index = jnp.arange(OWNERS, dtype=jnp.int32)[None, :]
    return jnp.where(owner_index == full_owner, most, counts).astype(jnp.int32)


def draw_leaf_inv(key, part):
    return lower_blocks(jax.random.fold_in(key, 11), LAYERS * LEAVES).reshape(LAYERS, LEAVES, BS, BS)


def draw_par_inv(key, part):
    return lower_blocks(jax.random.fold_in(key, 12), LAYERS * PARENTS).reshape(LAYERS, PARENTS, BS, BS)


def draw_top_inv(key, part):
    return lower_blocks(jax.random.fold_in(key, 13), TOP)


def draw_leaf_count(key, part):
    return list_counts(jax.random.fold_in(key, 21), LT_DEV)


def draw_par_count(key, part):
    return list_counts(jax.random.fold_in(key, 22), PT_DEV)


def draw_leaf_rows(key, part):
    first, second, third, fourth = jax.random.split(jax.random.fold_in(key, 31), 4)
    shape = (LAYERS, LT_ALL)
    owner = (jnp.arange(LT_ALL, dtype=jnp.int32) // LT_DEV)[None, :]
    groups = OWNERS // 8
    member = jax.random.randint(first, shape, 0, 8)
    target_owner = owner // 2 % groups * 2 + member % 2 + member // 2 * 2 * groups
    parent = target_owner * PAR_DEV + jax.random.randint(second, shape, 0, PAR_DEV)
    upper = PARENTS + jax.random.randint(third, shape, 0, TOP)
    picker = jax.random.randint(fourth, shape, 0, 2)
    return jnp.where(picker == 0, parent, upper).astype(jnp.int32)


def place_ends(drawn, rng, smallest, largest):
    spot = [jax.random.randint(jax.random.fold_in(rng, axis), (), 0, length) for axis, length in enumerate(drawn.shape)]
    widest = drawn.shape.index(max(drawn.shape))
    next_to = spot[:widest] + [(spot[widest] + 1) % drawn.shape[widest]] + spot[widest + 1:]
    return drawn.at[tuple(spot)].set(smallest).at[tuple(next_to)].set(largest)


def levels(own_key, shape, pieces, smallest, top_value):
    factor_of = 1.0
    for axis_at, blocks in pieces:
        draws = jax.random.uniform(jax.random.fold_in(jax.random.fold_in(own_key, 6), axis_at), (blocks,), jnp.float32, smallest / len(pieces), top_value / len(pieces))
        factor_of = factor_of * jnp.repeat(jnp.exp(draws), shape[axis_at] // blocks).reshape((-1,) + (1,) * (len(shape) - 1 - axis_at))
    return factor_of


def bell_draw(key, dims, width, limit, pieces=(), held_as=jnp.bfloat16):
    loudness = levels(key, dims, pieces, -0.22, 0.18) if pieces else 1.0
    values = jax.random.normal(key, dims, jnp.float32) * width * loudness
    return jnp.minimum(jnp.maximum(values, -limit), limit).astype(held_as)


def setup_inputs(seed: int = 0) -> dict:
    streams_of = jax.random.split(jax.random.key(seed), 15)
    leaf_rhs = bell_draw(streams_of[0], (LAYERS, LEAVES, BS, NRHS), 1.0, 6.0, ((0, 4), (1, 8)), jnp.float32)
    leaf_inv = draw_leaf_inv(jax.random.fold_in(streams_of[14], 71), 0)
    par_rhs = bell_draw(streams_of[2], (LAYERS, PARENTS, BS, NRHS), 1.0, 6.0, ((0, 4), (1, 8)), jnp.float32)
    par_inv = draw_par_inv(jax.random.fold_in(streams_of[14], 71), 0)
    top_rhs = bell_draw(streams_of[4], (TOP, BS, NRHS), 1.0, 6.0, ((0, 8), (2, 4)), jnp.float32)
    top_inv = draw_top_inv(jax.random.fold_in(streams_of[14], 71), 0)
    leaf_tiles = bell_draw(streams_of[6], (LAYERS, LT_ALL, BS, BS), (BS * 16) ** -0.5, 0.125, ((0, 4), (1, 8)), jnp.float32)
    leaf_cols = place_ends(jax.random.randint(streams_of[7], (LAYERS, LT_ALL), 0, LEAF_DEV), jax.random.fold_in(streams_of[7], 1), 0, LEAF_DEV - 1).astype(jnp.int32)
    leaf_rows = draw_leaf_rows(jax.random.fold_in(streams_of[14], 71), 0)
    leaf_count = draw_leaf_count(jax.random.fold_in(streams_of[14], 71), 0)
    par_tiles = bell_draw(streams_of[10], (LAYERS, PT_ALL, BS, BS), (BS * 16) ** -0.5, 0.125, ((0, 4), (1, 8)), jnp.float32)
    par_cols = place_ends(jax.random.randint(streams_of[11], (LAYERS, PT_ALL), 0, PAR_DEV), jax.random.fold_in(streams_of[11], 1), 0, PAR_DEV - 1).astype(jnp.int32)
    par_rows = place_ends(jax.random.randint(streams_of[12], (LAYERS, PT_ALL), 0, TOP), jax.random.fold_in(streams_of[12], 1), 0, TOP - 1).astype(jnp.int32)
    par_count = draw_par_count(jax.random.fold_in(streams_of[14], 71), 0)
    return {"leaf_rhs": leaf_rhs, "leaf_inv": leaf_inv, "par_rhs": par_rhs, "par_inv": par_inv, "top_rhs": top_rhs, "top_inv": top_inv, "leaf_tiles": leaf_tiles, "leaf_cols": leaf_cols, "leaf_rows": leaf_rows, "leaf_count": leaf_count, "par_tiles": par_tiles, "par_cols": par_cols, "par_rows": par_rows, "par_count": par_count}


def spread_update(tiles, cols, rows, count, solved, src_dev, per_dev, targets):
    highest = lax.Precision.HIGHEST
    tiles_owned = tiles.reshape(OWNERS, per_dev, BS, BS)
    cols_owned = cols.reshape(OWNERS, per_dev)
    rows_owned = rows.reshape(OWNERS, per_dev)

    def advance(total, item):
        tile_block, col_block, row_block, owner_count, owner = item
        source = owner * src_dev + col_block
        picked = jnp.take(solved, source.astype(jnp.int32), axis=0)
        product = jnp.einsum("tij,tjk->tik", tile_block, picked, precision=highest)
        in_use = jnp.arange(per_dev, dtype=jnp.int32) < owner_count
        product = jnp.where(in_use[:, None, None], product, jnp.zeros_like(product))
        return total + jax.ops.segment_sum(product, row_block, targets), None

    start = jnp.zeros((targets, BS, NRHS), jnp.float32)
    total, _ = lax.scan(advance, start, (tiles_owned, cols_owned, rows_owned, count, jnp.arange(OWNERS, dtype=jnp.int32)))
    return total


def reference(leaf_rhs, leaf_inv, par_rhs, par_inv, top_rhs, top_inv, leaf_tiles, leaf_cols, leaf_rows, leaf_count, par_tiles, par_cols, par_rows, par_count):
    highest = lax.Precision.HIGHEST
    ancestor = jnp.zeros((TOP, BS, NRHS), jnp.float32)
    parent_list = []
    for layer in range(LAYERS):
        leaf_solution = jnp.einsum("bij,bjk->bik", leaf_inv[layer], leaf_rhs[layer], precision=highest)
        leaf_update = spread_update(leaf_tiles[layer], leaf_cols[layer], leaf_rows[layer], leaf_count[layer], leaf_solution, LEAF_DEV, LT_DEV, PARENTS + TOP)
        parent_solution = jnp.einsum("bij,bjk->bik", par_inv[layer], par_rhs[layer] - leaf_update[:PARENTS], precision=highest)
        par_update = spread_update(par_tiles[layer], par_cols[layer], par_rows[layer], par_count[layer], parent_solution, PAR_DEV, PT_DEV, TOP)
        ancestor = ancestor + (leaf_update[PARENTS:] + par_update)
        parent_list.append(parent_solution)
    top_solution = jnp.einsum("bij,bjk->bik", top_inv, top_rhs - ancestor, precision=highest)
    return jnp.stack(parent_list), top_solution
```

```python
import functools
import math

import jax
import jax.numpy as jnp
from jax import lax
from jax.experimental import pallas as pl
from jax.experimental.pallas import tpu as pltpu
from jax.sharding import PartitionSpec as P

F32 = jnp.float32
BF16 = jnp.bfloat16


def split(value):
    high = value.astype(BF16)
    low = (value - high.astype(F32)).astype(BF16)
    return high, low


def dot(left, right):
    return jnp.dot(left, right, preferred_element_type=F32)


def dot3(left, right):
    left_high, left_low = left
    right_high, right_low = right
    return dot(left_high, right_high) + (dot(left_high, right_low) + dot(left_low, right_high))


def bits_of(number):
    bits = number.bit_length() - 1
    assert 1 << bits == number
    return bits


def slot_of(target, me, owners, per):
    owner = lax.div(target, jnp.int32(per))
    place = lax.rem(target, jnp.int32(per))
    relative = owner ^ me
    core = relative & 1
    rest = relative >> 1
    width = bits_of(owners) - 1
    turned = jnp.int32(0)
    for bit in range(width):
        turned = turned | (((rest >> bit) & 1) << (width - 1 - bit))
    where = jnp.where(place < per // 2, turned, rest)
    return (core * per + place) * (owners // 2) + where


def chunk_of(slots):
    return max(size for size in range(1, 17) if slots % size == 0)


def accumulate(rows_ref, cols_ref, count, first, number, me, owners, per, tiles_hbm, buf, acc, sems):
    slots = buf.shape[0]
    chunk = chunk_of(slots)

    def batch(g, _):
        @pl.when(g * chunk < count)
        def _():
            part = pl.ds(g * chunk, chunk)
            pltpu.make_async_copy(tiles_hbm.at[0, part], buf.at[part], sems.at[g]).wait()

            def one(s, _):
                row = rows_ref[0, s] - first

                @pl.when(jnp.logical_and(row >= 0, row < number))
                def _():
                    slot = slot_of(row, me, owners, per)
                    col = cols_ref[0, s]
                    acc[slot, col] = acc[slot, col] + buf[s]

                return 0

            lax.fori_loop(g * chunk, jnp.minimum((g + 1) * chunk, count), one, 0)

        return 0

    lax.fori_loop(0, slots // chunk, batch, 0)


def start_tiles(count, tiles_hbm, buf, sems):
    slots = buf.shape[0]
    chunk = chunk_of(slots)
    for g in range(slots // chunk):
        @pl.when(g * chunk < count)
        def _():
            part = pl.ds(g * chunk, chunk)
            pltpu.make_async_copy(tiles_hbm.at[0, part], buf.at[part], sems.at[g]).start()


def clear(acc):
    def one(k, _):
        acc[k] = jnp.zeros(acc.shape[1:], F32)
        return 0

    lax.fori_loop(0, acc.shape[0], one, 0)


def leaf_kernel(first, number, owners, per, me_ref, rows_ref, cols_ref, count_ref, inv_hbm, rhs_hbm, tiles_hbm,
                send_ref, keep_ref, buf, acc, inv, rhs, x_high, x_low, a_high, a_low, sems, small_sems):
    me = me_ref[0]
    count = count_ref[0, 0]
    inv_copy = pltpu.make_async_copy(inv_hbm.at[0], inv, small_sems.at[0])
    rhs_copy = pltpu.make_async_copy(rhs_hbm.at[0], rhs, small_sems.at[1])
    inv_copy.start()
    rhs_copy.start()
    start_tiles(count, tiles_hbm, buf, sems)
    clear(acc)
    inv_copy.wait()
    rhs_copy.wait()
    sources, block, _ = inv.shape
    for b in range(sources):
        high, low = split(dot3(split(inv[b]), split(rhs[b])))
        x_high[b * block:(b + 1) * block] = high
        x_low[b * block:(b + 1) * block] = low
    accumulate(rows_ref, cols_ref, count, first, number, me, owners, per, tiles_hbm, buf, acc, sems)
    group = a_high.shape[0] // block
    half = number // 2
    for side, out in ((1, send_ref), (0, keep_ref)):
        def some(g, _):
            for k in range(group):
                for b in range(sources):
                    high, low = split(acc[side * half + g * group + k, b])
                    a_high[k * block:(k + 1) * block, b * block:(b + 1) * block] = high
                    a_low[k * block:(k + 1) * block, b * block:(b + 1) * block] = low
            product = dot3((a_high[...], a_low[...]), (x_high[...], x_low[...]))
            out[pl.ds(g * group, group)] = product.reshape(group, block, -1)
            return 0

        lax.fori_loop(0, half // group, some, 0)


def whole(count):
    return [pl.BlockSpec(memory_space=pltpu.VMEM)] * count


def scalars(count):
    return [pl.BlockSpec(memory_space=pltpu.SMEM)] * count


def hbm(count):
    return [pl.BlockSpec(memory_space=pl.ANY)] * count


def leaf_products(me, rows, cols, count, inv, rhs, tiles, first, number, owners, per, name):
    slots, block = tiles.shape[1], tiles.shape[2]
    sources, columns = rhs.shape[1], rhs.shape[3]
    half = number // 2
    group = math.gcd(half, 4)
    out = jax.ShapeDtypeStruct((half, block, columns), F32)
    flops = 6 * number * block * sources * block * columns
    vmem = 4 * block * block * (slots + (number + 4) * sources) + 12 * number * block * columns + (6 << 20)
    return pl.pallas_call(
        functools.partial(leaf_kernel, first, number, owners, per),
        name=name,
        out_shape=(out, out),
        in_specs=scalars(4) + hbm(3),
        out_specs=tuple(whole(2)),
        scratch_shapes=[
            pltpu.VMEM((slots, block, block), F32),
            pltpu.VMEM((number, sources, block, block), F32),
            pltpu.VMEM(inv.shape[1:], F32),
            pltpu.VMEM(rhs.shape[1:], F32),
            pltpu.VMEM((sources * block, columns), BF16),
            pltpu.VMEM((sources * block, columns), BF16),
            pltpu.VMEM((group * block, sources * block), BF16),
            pltpu.VMEM((group * block, sources * block), BF16),
            pltpu.SemaphoreType.DMA((slots // chunk_of(slots),)),
            pltpu.SemaphoreType.DMA((2,)),
        ],
        compiler_params=pltpu.CompilerParams(vmem_limit_bytes=min(vmem, 60 << 20)),
        cost_estimate=pl.CostEstimate(flops=flops, bytes_accessed=tiles.size * 4, transcendentals=0),
    )(me, rows, cols, count, inv, rhs, tiles)


def parent_sum_kernel(number, owners, per, me_ref, rows_ref, cols_ref, count_ref, tiles_hbm, top_inv_ref, top_rhs_ref,
                      high_ref, low_ref, base_ref, buf, acc, sems):
    me = me_ref[0]
    count = count_ref[0, 0]
    start_tiles(count, tiles_hbm, buf, sems)
    clear(acc)
    for t in range(top_inv_ref.shape[0]):
        left = split(top_inv_ref[t])
        base_ref[t] = dot3(left, split(top_rhs_ref[t].T)).T
    accumulate(rows_ref, cols_ref, count, 0, number, me, owners, per, tiles_hbm, buf, acc, sems)
    sources, block = acc.shape[1], acc.shape[2]

    def one(k, _):
        for b in range(sources):
            high, low = split(acc[k, b])
            high_ref[k, :, b * block:(b + 1) * block] = high
            low_ref[k, :, b * block:(b + 1) * block] = low
        return 0

    lax.fori_loop(0, number, one, 0)


def parent_sums(me, rows, cols, count, tiles, top_inv, top_rhs, sources, number, owners, per):
    slots, block = tiles.shape[1], tiles.shape[2]
    half = jax.ShapeDtypeStruct((number, block, sources * block), BF16)
    vmem = 4 * block * block * (slots + 2 * number * sources) + (6 << 20)
    return pl.pallas_call(
        functools.partial(parent_sum_kernel, number, owners, per),
        name="parent_sums",
        out_shape=(half, half, jax.ShapeDtypeStruct(top_rhs.shape, F32)),
        in_specs=scalars(4) + hbm(1) + whole(2),
        out_specs=tuple(whole(3)),
        scratch_shapes=[
            pltpu.VMEM((slots, block, block), F32),
            pltpu.VMEM((number, sources, block, block), F32),
            pltpu.SemaphoreType.DMA((slots // chunk_of(slots),)),
        ],
        compiler_params=pltpu.CompilerParams(vmem_limit_bytes=min(vmem, 60 << 20)),
        cost_estimate=pl.CostEstimate(flops=tiles.size, bytes_accessed=tiles.size * 4, transcendentals=0),
    )(me, rows, cols, count, tiles, top_inv, top_rhs)


def parent_kernel(parts, rhs_ref, inv_ref, high_ref, low_ref, send_leaf_ref, keep_leaf_ref, *refs):
    pieces, (solution_ref, send_ref, keep_ref, p_high, p_low) = refs[:2 * parts], refs[2 * parts:]
    per, block, _ = rhs_ref.shape
    place = 0
    for part in range(parts):
        mine, other = pieces[2 * part], pieces[2 * part + 1]
        for k in range(mine.shape[0]):
            right = rhs_ref[place] - (mine[k] + other[k])
            solved = dot3(split(inv_ref[place]), split(right))
            solution_ref[place] = solved
            high, low = split(solved)
            p_high[place * block:(place + 1) * block] = high
            p_low[place * block:(place + 1) * block] = low
            place += 1
    half = send_ref.shape[0]
    group = math.gcd(half, 4)
    for side, leaf, out in ((1, send_leaf_ref, send_ref), (0, keep_leaf_ref, keep_ref)):
        def some(g, _):
            part = pl.ds(side * half + g * group, group)
            high = high_ref[part].reshape(group * block, -1)
            low = low_ref[part].reshape(group * block, -1)
            product = dot3((high, low), (p_high[...], p_low[...]))
            here = pl.ds(g * group, group)
            out[here] = leaf[here] + product.reshape(group, block, -1)
            return 0

        lax.fori_loop(0, half // group, some, 0)


def parent_products(rhs, inv, high, low, send_leaf, keep_leaf, pieces):
    per, block, columns = rhs.shape
    out = jax.ShapeDtypeStruct(send_leaf.shape, F32)
    flops = 6 * high.size * columns
    return pl.pallas_call(
        functools.partial(parent_kernel, len(pieces) // 2),
        name="parent_products",
        out_shape=(jax.ShapeDtypeStruct(rhs.shape, F32), out, out),
        in_specs=whole(6 + len(pieces)),
        out_specs=tuple(whole(3)),
        scratch_shapes=[pltpu.VMEM((per * block, columns), BF16)] * 2,
        compiler_params=pltpu.CompilerParams(vmem_limit_bytes=(8 << 20) + 16 * send_leaf.size + 4 * high.size),
        cost_estimate=pl.CostEstimate(flops=flops, bytes_accessed=4 * high.size, transcendentals=0),
    )(rhs, inv, high, low, send_leaf, keep_leaf, *pieces)


def top_kernel(parts, layers, layer_ref, inv_ref, *refs):
    pieces, (out_ref, turned) = refs[:2 * parts], refs[2 * parts:]
    width = out_ref.shape[2]
    layer = layer_ref[0]
    place = 0
    for part in range(parts):
        mine, other = pieces[2 * part], pieces[2 * part + 1]
        for k in range(mine.shape[0]):
            turned[...] = dot3(split(inv_ref[place]), split(mine[k] + other[k])).T
            for d in range(layers):
                start = pl.multiple_of((layer ^ d) * width, width)
                out_ref[d, place] = turned[pl.ds(start, width)]
            place += 1


def top_products(layer, inv, pieces, layers):
    per, block, _ = inv.shape
    columns = pieces[0].shape[2]
    return pl.pallas_call(
        functools.partial(top_kernel, len(pieces) // 2, layers),
        name="top_products",
        out_shape=jax.ShapeDtypeStruct((layers, per, columns // layers, block), F32),
        in_specs=scalars(1) + whole(1 + len(pieces)),
        out_specs=whole(1)[0],
        scratch_shapes=[pltpu.VMEM((columns, block), F32)],
        compiler_params=pltpu.CompilerParams(vmem_limit_bytes=8 << 20),
        cost_estimate=pl.CostEstimate(flops=6 * inv.size * columns, bytes_accessed=inv.size * 4, transcendentals=0),
    )(layer, inv, *pieces)


def exchange(value, axis, mask):
    size = lax.axis_size(axis)
    return lax.ppermute(value, axis, [(i, i ^ mask) for i in range(size)])


def scatter_sum(send, keep, owners, per):
    got = exchange(send, "tile", 1)
    rest = owners // 2
    halves = [(0, per // 2), (per // 2, per)] if per > 1 else [(0, per)]
    orders = [[1 << bit for bit in range(1, bits_of(owners))]]
    orders.append(orders[0][::-1])
    if per == 1:
        orders = orders[1:]
    shape = (per, rest) + send.shape[1:]
    keep, got = keep.reshape(shape), got.reshape(shape)
    state = []
    for low, high in halves:
        state.append((keep[low:high], got[low:high]))
    for step in range(bits_of(rest)):
        sent = []
        for (mine, other), order in zip(state, orders):
            cut = mine.shape[1] // 2
            sent.append(exchange(mine[:, cut:] + other[:, cut:], "tile", order[step]))
        state = [
            (mine[:, : mine.shape[1] // 2] + other[:, : mine.shape[1] // 2], new)
            for (mine, other), new in zip(state, sent)
        ]
    pieces = []
    for mine, other in state:
        pieces += [mine[:, 0], other[:, 0]]
    return pieces


def local(leaf_rhs, leaf_inv, par_rhs, par_inv, top_rhs, top_inv, leaf_tiles, leaf_cols, leaf_rows, leaf_count,
          par_tiles, par_cols, par_rows, par_count):
    owners, layers = lax.axis_size("tile"), lax.axis_size("layer")
    per, top_per = par_rhs.shape[1], top_inv.shape[0]
    parents, tops = per * owners, top_per * owners
    me = lax.axis_index("tile").astype(jnp.int32).reshape(1)
    layer = lax.axis_index("layer").astype(jnp.int32).reshape(1)
    leaf = (me, leaf_rows, leaf_cols, leaf_count, leaf_inv, leaf_rhs, leaf_tiles)
    send, keep = leaf_products(*leaf, 0, parents, owners, per, "leaf_to_parents")
    pieces = scatter_sum(send, keep, owners, per)
    send_leaf, keep_leaf = leaf_products(*leaf, parents, tops, owners, top_per, "leaf_to_tops")
    top_rhs_turned = jnp.transpose(top_rhs, (0, 2, 1))
    high, low, base = parent_sums(
        me, par_rows, par_cols, par_count, par_tiles, top_inv, top_rhs_turned, per, tops, owners, top_per
    )
    solved, send, keep = parent_products(par_rhs[0], par_inv[0], high, low, send_leaf, keep_leaf, pieces)
    pieces = scatter_sum(send, keep, owners, top_per)
    chunks = top_products(layer, top_inv, pieces, layers)
    total = base - chunks[0]
    others = [exchange(chunks[d], "layer", d) for d in range(1, layers)]
    for other in others:
        total = total - other
    return solved[None], jnp.transpose(total, (0, 2, 1))


def solution(mesh):
    spread = P("layer", "tile", None, None)
    lists = P("layer", "tile")
    in_specs = (spread, spread, spread, spread, P("tile", None, "layer"), P("tile", None, None), spread, lists, lists,
                lists, spread, lists, lists, lists)
    out_specs = (spread, P("tile", None, "layer"))
    return jax.shard_map(local, mesh=mesh, in_specs=in_specs, out_specs=out_specs, check_vma=False)
```
